256 devices in a mesh: seq: 8 (over y, core), tensor: 32 (over z, x).
Axes of the slice: x: 4, y: 4, z: 8, core: 2. Of those that a mesh axis runs over, the one named last changes fastest.
Arguments:
- tokens: bfloat16 [4096, 3584], P('seq', 'tensor'), may hold values from -6 to 6
- w_zx: bfloat16 [2, 3584, 4096], P(None, None, 'tensor'), may hold values from -0.09375 to 0.09375
- w_bc: bfloat16 [3584, 128], replicated, may hold values from -0.09375 to 0.09375
- w_dt: bfloat16 [3584, 64], P(None, 'tensor'), may hold values from -0.09375 to 0.09375
- dt_bias: float32 [64], P('tensor'), may hold values from -2 to 0.5
- a_rate: float32 [64], P('tensor'), may hold values from 0.00012207031 to 0.05
- d_skip: float32 [64], P('tensor'), may hold values from 0.3 to 1.5
- conv_x: float32 [4, 4096], P(None, 'tensor'), may hold values from -3 to 3
- conv_bc: float32 [4, 128], replicated, may hold values from -3 to 3
- norm_gain: float32 [4096], P('tensor'), may hold values from 0.25 to 1.75
- w_out: bfloat16 [4096, 3584], P('tensor'), may hold values from -0.09375 to 0.09375
- segments: int32 [4096], P('seq'), may hold values from 0 to 5, never falling along the last dimension, each value on 1 to 2048 neighbouring positions
Outputs:
- mixed: bfloat16 [4096, 3584], P(('seq', 'tensor'))
The draws below stay inside these ranges and needn't reach their ends.
Inputs may be any that keep to these rules, and one draw needn't show every extreme that they name: `segments`: prompt ids never fall along the tokens, so each prompt's tokens are contiguous.
All inputs are finite; a program needn't handle non-finite values.
Results may differ from the reference program's by a relative error of at most 0.02.
Values may be sent and summed in bfloat16 or wider, within the bound.
A program may use at most 64 MiB of HBM per device.

```python
import math
import jax
import jax.numpy as jnp
import numpy as np
from jax import lax

D = 3584
P_SIZE = 64
N = 64
KCONV = 4
BLOCK = 256
HEAD_DEV = 2
SEGS = 6
HEADS = 64
TOKENS = 4096


def level_of(key, extent, shards, least, top_value):
    gain, own = 1.0, jax.random.fold_in(key, 6)
    for axis_at, shards_of in shards:
        draws = jnp.exp(jax.random.uniform(jax.random.fold_in(own, axis_at), (shards_of,), jnp.float32, least / len(shards), top_value / len(shards)))
        gain = gain * jnp.repeat(draws, extent[axis_at] // shards_of).reshape([-1 if axis == axis_at else 1 for axis in range(len(extent))])
    return gain


def length_profile(amount, total, reach, slope):
    weights = [(1 << 20) // math.isqrt(rank ** slope) + 1 for rank in range(2, amount + 1)]
    surplus, holding = total - reach - (amount - 1), [1] * (amount - 1)
    while surplus > 0:
        movable = [i for i in range(amount - 1) if holding[i] < reach]
        pool, budget = sum([weights[i] for i in movable]), surplus
        for i in movable:
            addition = min(reach - holding[i], max(1, budget * weights[i] // pool), surplus)
            holding[i] = holding[i] + addition
            surplus = surplus - addition
    return np.array([reach] + holding)


def uneven(own_key, count, total, limit, slope):
    if count == 2:
        one = jax.random.randint(own_key, (), max(1, total - limit), min(limit, total - 1) + 1)
        return jnp.stack([one, total - one])
    lengths = jnp.asarray(length_profile(count, total, limit, slope), jnp.int32)
    couples = (count - 1) // 2
    donor, receiver = lengths[1:1 + 2 * couples:2], lengths[2:2 + 2 * couples:2]
    margin = jnp.minimum(donor - 1, limit - receiver)
    passed = jax.random.randint(jax.random.fold_in(own_key, 1), (couples,), 0, 1 << 20) % (margin + 1)
    lengths = lengths.at[1:1 + 2 * couples:2].set(donor - passed).at[2:2 + 2 * couples:2].set(receiver + passed)
    return lengths[jax.random.permutation(jax.random.fold_in(own_key, 2), count)]


def scatter_about(own_key, dims, spread, limit, cuts=(), kind=jnp.bfloat16):
    result = spread * jax.random.normal(own_key, dims, jnp.float32)
    if cuts:
        result = result * level_of(own_key, dims, cuts, -0.22, 0.18)
    return jnp.clip(result, -limit, limit).astype(kind)


def setup_inputs(seed: int = 0) -> dict:
    streams_of = jax.random.split(jax.random.key(seed), 13)
    tokens = scatter_about(streams_of[0], (TOKENS, D), 1.0, 6.0, ((0, 8), (1, 32)))
    w_zx = scatter_about(streams_of[1], (2, D, HEADS * P_SIZE), D ** -0.5, 0.09375, ((2, 32),))
    w_bc = scatter_about(streams_of[2], (D, 2 * N), D ** -0.5, 0.09375)
    w_dt = scatter_about(streams_of[3], (D, HEADS), D ** -0.5, 0.09375, ((1, 32),))
    dt_bias = jnp.clip(-2.0 + 2.5 * jax.random.uniform(streams_of[4], (HEADS,), jnp.float32) ** level_of(streams_of[4], (HEADS,), ((0, 32),), -0.2, 0.2), -2.0, 0.5)
    a_rate = jnp.clip(jnp.exp(math.log(0.05) - 6.015181 * jax.random.uniform(streams_of[5], (HEADS,), jnp.float32) ** level_of(streams_of[5], (HEADS,), ((0, 32),), -0.2, 0.2)), 0.00012207031, 0.05)
    d_skip = jnp.clip(0.3 + 1.2 * jax.random.uniform(streams_of[6], (HEADS,), jnp.float32) ** level_of(streams_of[6], (HEADS,), ((0, 32),), -0.2, 0.2), 0.3, 1.5)
    conv_x = scatter_about(streams_of[7], (KCONV, HEADS * P_SIZE), 0.5, 3.0, ((1, 32),), jnp.float32)
    conv_bc = scatter_about(streams_of[8], (KCONV, 2 * N), 0.5, 3.0, (), jnp.float32)
    norm_gain = jnp.clip(1.0 + 0.15 * jax.random.normal(streams_of[9], (HEADS * P_SIZE,), jnp.float32), 0.25, 1.75)
    w_out = scatter_about(streams_of[10], (HEADS * P_SIZE, D), (HEADS * P_SIZE) ** -0.5, 0.09375, ((0, 32),))
    segments = jnp.searchsorted(jnp.cumsum(uneven(streams_of[11], SEGS, TOKENS, TOKENS // 2, 2)), jnp.arange(TOKENS), side="right").astype(jnp.int32)
    return {"tokens": tokens, "w_zx": w_zx, "w_bc": w_bc, "w_dt": w_dt, "dt_bias": dt_bias, "a_rate": a_rate, "d_skip": d_skip, "conv_x": conv_x, "conv_bc": conv_bc, "norm_gain": norm_gain, "w_out": w_out, "segments": segments}


HIGHEST_PREC = lax.Precision.HIGHEST
NORM_EPS = 1e-05

def conv_tail(extended, seg_ext, taps, tok_rows):
    conv_len = taps.shape[0]
    seg_now = seg_ext[conv_len - 1:]
    conv_sum = taps[conv_len - 1] * extended[conv_len - 1:]
    for offset in range(1, conv_len):
        earlier = extended[conv_len - 1 - offset:conv_len - 1 - offset + tok_rows]
        seg_then = seg_ext[conv_len - 1 - offset:conv_len - 1 - offset + tok_rows]
        conv_sum = conv_sum + taps[conv_len - 1 - offset] * jnp.where((seg_then == seg_now)[:, None], earlier, 0.0)
    return jax.nn.silu(conv_sum)

def ssd_block(carry, block):
    state, last_seg = carry
    inner_x, step_size, logdec, bmat, cmat, seg_ids = block
    cum_decay = jnp.cumsum(logdec, axis=0)
    position = jnp.arange(seg_ids.shape[0])
    visible = (seg_ids[:, None] == seg_ids[None, :]) & (position[:, None] >= position[None, :])
    gap_decay = jnp.where(visible[:, :, None], cum_decay[:, None, :] - cum_decay[None, :, :], -jnp.inf)
    scores = jnp.dot(cmat, bmat.T, precision=HIGHEST_PREC)
    weights = jnp.exp(gap_decay) * scores[:, :, None] * step_size[None, :, :]
    block_out = jnp.einsum('tsh,shp->thp', weights, inner_x, precision=HIGHEST_PREC)
    enter = jnp.where((seg_ids == last_seg)[:, None], jnp.exp(cum_decay), 0.0)
    block_out = block_out + enter[:, :, None] * jnp.einsum('tn,hpn->thp', cmat, state, precision=HIGHEST_PREC)
    tail_weight = jnp.where((seg_ids == seg_ids[-1])[:, None], jnp.exp(cum_decay[-1][None, :] - cum_decay), 0.0) * step_size
    carry_keep = jnp.where(seg_ids[-1] == last_seg, jnp.exp(cum_decay[-1]), 0.0)
    new_state = carry_keep[:, None, None] * state + jnp.einsum('sh,shp,sn->hpn', tail_weight, inner_x, bmat, precision=HIGHEST_PREC)
    return ((new_state, seg_ids[-1]), block_out)

def add_partial(total, group):
    normed_part, weight_part = group
    partial_value = jnp.dot(normed_part, weight_part, preferred_element_type=jnp.float32).astype(jnp.bfloat16)
    partial_value = lax.optimization_barrier(partial_value)
    return (total + partial_value.astype(jnp.float32), None)

def reference(tokens, w_zx, w_bc, w_dt, dt_bias, a_rate, d_skip, conv_x, conv_bc, norm_gain, w_out, segments):
    gate_proj = jnp.dot(tokens, w_zx[0], preferred_element_type=jnp.float32).astype(jnp.bfloat16)
    inner_proj = jnp.dot(tokens, w_zx[1], preferred_element_type=jnp.float32).astype(jnp.bfloat16)
    bc_proj = jnp.dot(tokens, w_bc, preferred_element_type=jnp.float32).astype(jnp.bfloat16)
    dt_raw = jnp.dot(tokens, w_dt, preferred_element_type=jnp.float32)
    rim_len = KCONV - 1
    seg_ext = jnp.concatenate([jnp.full((rim_len,), -1, jnp.int32), segments.astype(jnp.int32)], 0)
    conv_inner = conv_tail(jnp.concatenate([jnp.zeros((rim_len, HEADS * P_SIZE), jnp.float32), inner_proj.astype(jnp.float32)], 0), seg_ext, conv_x, TOKENS)
    conv_state = conv_tail(jnp.concatenate([jnp.zeros((rim_len, 2 * N), jnp.float32), bc_proj.astype(jnp.float32)], 0), seg_ext, conv_bc, TOKENS)
    bmat = conv_state[:, :N]
    cmat = conv_state[:, N:]
    step_size = jax.nn.softplus(dt_raw + dt_bias)
    logdec = -a_rate * step_size
    inner_heads = conv_inner.reshape(TOKENS, HEADS, P_SIZE)
    nblocks = TOKENS // BLOCK
    blocks = (inner_heads.reshape(nblocks, BLOCK, HEADS, P_SIZE), step_size.reshape(nblocks, BLOCK, HEADS), logdec.reshape(nblocks, BLOCK, HEADS), bmat.reshape(nblocks, BLOCK, N), cmat.reshape(nblocks, BLOCK, N), segments.astype(jnp.int32).reshape(nblocks, BLOCK))
    start = (jnp.zeros((HEADS, P_SIZE, N), jnp.float32), jnp.array(-1, jnp.int32))
    _, block_outs = lax.scan(ssd_block, start, blocks)
    ssd_out = block_outs.reshape(TOKENS, HEADS, P_SIZE) + d_skip[None, :, None] * inner_heads
    gated = ssd_out.reshape(TOKENS, HEADS * P_SIZE) * jax.nn.silu(gate_proj.astype(jnp.float32))
    scale = lax.rsqrt(lax.optimization_barrier(jnp.mean(gated * gated, axis=1)) + NORM_EPS)
    normed = (gated * scale[:, None] * norm_gain).astype(jnp.bfloat16)
    groups = HEADS // HEAD_DEV
    group_w = HEAD_DEV * P_SIZE
    normed_groups = jnp.transpose(normed.reshape(TOKENS, groups, group_w), (1, 0, 2))
    weight_groups = w_out.reshape(groups, group_w, D)
    total, _ = lax.scan(add_partial, jnp.zeros((TOKENS, D), jnp.float32), (normed_groups, weight_groups))
    return total.astype(jnp.bfloat16)
```

```python
import jax
import jax.numpy as jnp
from jax import lax
from jax.experimental import pallas as pl
from jax.experimental.pallas import tpu as pltpu
from jax.sharding import PartitionSpec as P

NORM_EPS = 1e-05
TOK = 512
FEAT = 112
DEPTH = 3584
QUART = DEPTH // 4
WIDE = DEPTH + 128
HALF = 256
MESH = pl.DeviceIdType.MESH
F32 = jnp.float32
BF16 = jnp.bfloat16


def silu(v):
    return v / (1.0 + jnp.exp(-v))


def softplus(v):
    return jnp.maximum(v, 0.0) + jnp.log1p(jnp.exp(-jnp.abs(v)))


def dot_tn(a, b):
    return lax.dot_general(a, b, (((0,), (0,)), ((), ())), preferred_element_type=F32)


def dot_nt(a, b):
    return lax.dot_general(a, b, (((1,), (1,)), ((), ())), preferred_element_type=F32)


def dot_nn(a, b):
    return jnp.dot(a, b, preferred_element_type=F32)


def three_parts(v):
    hi = v.astype(BF16)
    rest = v - hi.astype(F32)
    mid = rest.astype(BF16)
    low = (rest - mid.astype(F32)).astype(BF16)
    return hi, mid, low


def kernel(
    tok_hbm, wzx_hbm, wbc_hbm, wdt_hbm, small_hbm, tapbc_ref, wout_hbm, seg_hbm,
    out_ref,
    G, WZ, WB, WD, SM, SEG, WO, ACC, LT, HXS, HXR, STS, STR, GN, PS,
    RXF, RXC, RXS, RZF, RZC, RZS, FS, FR,
    SS, RG, RW, RO, RM, RH, RS, RN, RF, RC, RX, RZ, LC,
):
    seq, ten = lax.axis_index("seq"), lax.axis_index("tensor")
    y, c = seq // 2, seq % 2
    z, x = ten // 4, ten % 4
    w, kap = z // 2, z % 2
    blk = 2 * y + kap
    sgn = 1 - 2 * c
    native = c == kap
    foreign = c != kap

    def m4(v):
        return (v + 8) % 4

    def dev(yy, zz, xx, cc):
        return (2 * yy + cc, 4 * zz + xx)

    core = dev(y, z, x, 1 - c)

    def dx(k):
        return dev(y, z, m4(x + k), c)

    def dw(k):
        return dev(y, 2 * m4(w + k) + kap, x, c)

    def dy(k):
        return dev(m4(y + k), z, x, c)

    other_z = z + 1 - 2 * kap
    swap = dev(y, other_z, x, 1 - c)
    twin = dev(y, other_z, x, c)

    def chain(b):
        return dev(b // 2, 2 * w + b % 2, x, c)

    count = [0]
    pending = []

    def send(src, dst, rsem, device, track=True):
        k = count[0]
        count[0] += 1
        cp = pltpu.make_async_remote_copy(
            src_ref=src, dst_ref=dst, send_sem=SS.at[k], recv_sem=rsem,
            device_id=device, device_id_type=MESH,
        )
        cp.start()
        if track:
            pending.append(cp)
        return cp

    def arrive(dst, rsem):
        pltpu.make_async_remote_copy(
            src_ref=dst, dst_ref=dst, send_sem=SS.at[0], recv_sem=rsem,
            device_id=core, device_id_type=MESH,
        ).wait_recv()

    def gslot(f):
        return G.at[pl.ds(pl.multiple_of(f * FEAT, 16), FEAT), :]

    def fid(wj, xj, cc):
        return 8 * m4(wj) + 4 * cc + m4(xj)

    def gsend(wj, xj, device):
        f = fid(wj, xj, c)
        send(gslot(f), gslot(f), RG.at[f], device)

    def gwait(wj, xj, cc):
        f = fid(wj, xj, cc)
        arrive(gslot(f), RG.at[f])

    def orow(par):
        return pl.ds(pl.multiple_of(128 * par, 128), 128)

    own_f = fid(w, x, c)
    l_wb = pltpu.make_async_copy(wbc_hbm, WB, LC.at[0])
    l_wo = pltpu.make_async_copy(wout_hbm, WO.at[orow(kap), :], LC.at[1])
    l_tok = pltpu.make_async_copy(tok_hbm, gslot(own_f), LC.at[2])
    l_wz = pltpu.make_async_copy(wzx_hbm, WZ, LC.at[3])
    l_wd = pltpu.make_async_copy(wdt_hbm, WD, LC.at[4])
    l_sm = pltpu.make_async_copy(small_hbm, SM, LC.at[5])
    l_sg = pltpu.make_async_copy(seg_hbm, SEG, LC.at[6])

    @pl.when(native)
    def _():
        l_tok.start()
        l_sg.start()
        l_wz.start()
        l_wd.start()
        l_sm.start()

    l_wb.start()
    l_wo.start()

    barrier = pltpu.get_barrier_semaphore()
    peers = [core, dx(1), dx(3), dw(1), dw(3), swap]
    peers += [chain((blk + k) % 8) for k in range(1, 8)]
    for p in peers:
        pl.semaphore_signal(barrier, inc=1, device_id=p, device_id_type=MESH)
    rows = lax.broadcasted_iota(jnp.int32, (TOK, TOK), 0)
    cols = lax.broadcasted_iota(jnp.int32, (TOK, TOK), 1)
    LT[...] = jnp.where(rows <= cols, 1.0, 0.0).astype(BF16)
    pl.semaphore_wait(barrier, len(peers))

    quart = pl.ds(pl.multiple_of(y * QUART, 128), QUART)

    def qrow(k):
        return pl.ds(pl.multiple_of(m4(y + k) * QUART, 128), QUART)

    k0 = count[0]
    count[0] += 4

    def sp_send(k, src, dst, rsem, device):
        return pltpu.make_async_remote_copy(
            src_ref=src, dst_ref=dst, send_sem=SS.at[k0 + k], recv_sem=rsem,
            device_id=device, device_id_type=MESH,
        )

    f_swap = fid(w, x, 1 - c)
    s_swap = sp_send(0, tok_hbm, gslot(f_swap), RG.at[f_swap], swap)
    s_seg = sp_send(0, seg_hbm, SEG, RM.at[2], core)
    s_wz = sp_send(1, wzx_hbm.at[:, quart, :], WZ.at[:, quart, :], RW.at[0], twin)
    s_wd = sp_send(2, wdt_hbm, WD, RM.at[0], twin)
    s_sm = sp_send(3, small_hbm, SM, RM.at[1], twin)

    @pl.when(foreign)
    def _():
        s_swap.start()
        gwait(w, x, c)

    @pl.when(native)
    def _():
        s_seg.start()
        l_tok.wait()

    gsend(w, x, dw(1))
    gsend(w, x, dw(3))
    gsend(w, x, dx(1))
    gsend(w, x, dx(3))
    gsend(w, x, core)

    @pl.when(native)
    def _():
        s_wd.start()
        s_sm.start()
        s_wz.start()

    def pass_x(wj):
        gwait(wj, x - sgn, c)
        gsend(wj, x - sgn, dx(sgn))
        gsend(wj, x - sgn, core)

    def spread_x(wj):
        gsend(wj, x, dx(1))
        gsend(wj, x, dx(3))
        gsend(wj, x, core)

    def to_core(wj, xj):
        gwait(wj, xj, c)
        gsend(wj, xj, core)

    pass_x(w)
    gwait(w - sgn, x, c)
    gsend(w - sgn, x, dw(sgn))
    spread_x(w - sgn)
    gwait(w + sgn, x, c)
    spread_x(w + sgn)
    to_core(w, x + sgn)

    kw = count[0]
    count[0] += 10

    def wsend(k, src, dst, rsem, device):
        return pltpu.make_async_remote_copy(
            src_ref=src, dst_ref=dst, send_sem=SS.at[kw + k], recv_sem=rsem,
            device_id=device, device_id_type=MESH,
        )

    def wz_at(k):
        return WZ.at[:, qrow(k), :]

    w_up = wsend(0, wz_at(0), wz_at(0), RW.at[1], dy(1))
    w_down = wsend(1, wz_at(0), wz_at(0), RW.at[2], dy(3))
    w_fg = wsend(2, WZ.at[0, qrow(-1), :], WZ.at[0, qrow(-1), :], RW.at[3], dy(1))
    w_fi = wsend(3, WZ.at[1, qrow(1), :], WZ.at[1, qrow(1), :], RW.at[4], dy(3))
    other = orow(1 - kap)

    def wo_at(k, lo=0, n=128):
        return WO.at[pl.ds(pl.multiple_of(128 * (1 - kap) + lo, 64), n), qrow(k)]

    o_first = wsend(
        4, wout_hbm.at[:, quart], WO.at[orow(kap), quart], RO.at[0], twin
    )
    o_up = wsend(4, wo_at(0), wo_at(0), RO.at[1], dy(1))
    o_down = wsend(5, wo_at(0), wo_at(0), RO.at[2], dy(3))
    o_fg = wsend(6, wo_at(-1, 0, 64), wo_at(-1, 0, 64), RO.at[3], dy(1))
    o_fi = wsend(7, wo_at(1, 64, 64), wo_at(1, 64, 64), RO.at[4], dy(3))
    o_core = wsend(8, WO.at[other, :], WO.at[other, :], RO.at[5], core)

    @pl.when(foreign)
    def _():
        arrive(wz_at(0), RW.at[0])
        w_up.start()
        w_down.start()

    pass_x(w - sgn)
    pass_x(w + sgn)
    gwait(w + 2, x, c)
    spread_x(w + 2)

    @pl.when(native)
    def _():
        o_first.start()

    to_core(w, x + 2)
    to_core(w - sgn, x + sgn)
    to_core(w + sgn, x + sgn)
    pass_x(w + 2)

    @pl.when(foreign)
    def _():
        arrive(wz_at(-1), RW.at[1])
        w_fg.start()
        arrive(wz_at(1), RW.at[2])
        w_fi.start()
        arrive(wo_at(0), RO.at[0])
        o_up.start()
        o_down.start()

    to_core(w - sgn, x + 2)
    to_core(w + sgn, x + 2)
    to_core(w + 2, x + sgn)
    to_core(w + 2, x + 2)

    @pl.when(foreign)
    def _():
        arrive(WZ.at[0, qrow(2), :], RW.at[3])
        arrive(WZ.at[1, qrow(2), :], RW.at[4])
        arrive(WD, RM.at[0])
        arrive(SM, RM.at[1])
        arrive(SEG, RM.at[2])

    @pl.when(native)
    def _():
        l_wz.wait()
        l_wd.wait()
        l_sm.wait()
        l_sg.wait()

    l_wb.wait()

    for i, wj in enumerate((w, w - sgn, w + sgn, w + 2)):
        for xj in range(4):
            gwait(wj, xj, 1 - c)
        krow = pl.ds(pl.multiple_of(m4(wj) * QUART, 128), QUART)
        gk = G[krow, :]
        parts = (
            dot_tn(WZ[0, krow, :], gk),
            dot_tn(WZ[1, krow, :], gk),
            dot_tn(WB[krow, :], gk),
        )
        for j, part in enumerate(parts):
            at = slice(128 * j, 128 * j + 128)
            ACC[at, :] = part if i == 0 else ACC[at, :] + part

    dt_raw = dot_nn(WD[...], G[...])

    @pl.when(foreign)
    def _():
        arrive(wo_at(-1), RO.at[1])
        o_fg.start()
        arrive(wo_at(1), RO.at[2])
        o_fi.start()

    seg = SEG[...].astype(F32)
    HXS[0:256, :] = ACC[128:384, TOK - 128:].astype(BF16)
    HXS[256:272, :] = jnp.broadcast_to(seg[:, TOK - 128:], (16, 128)).astype(BF16)
    kh = count[0]
    count[0] += 8
    h_send = pltpu.make_async_remote_copy(
        src_ref=HXS, dst_ref=HXR, send_sem=SS.at[kh], recv_sem=RH.at[0],
        device_id=chain((blk + 1) % 8), device_id_type=MESH,
    )

    @pl.when(blk < 7)
    def _():
        h_send.start()

    @pl.when(blk == 0)
    def _():
        HXR[0:256, :] = jnp.zeros((256, 128), BF16)
        HXR[256:272, :] = jnp.full((16, 128), -1.0, BF16)

    sm = SM[...]
    smt = jnp.concatenate([sm, jnp.zeros((120, 128), F32)], 0).T
    step = softplus(dt_raw + smt[0:2, 6:7])
    logdec = -smt[0:2, 7:8] * step
    hi, mid, low = three_parts(logdec)
    pieces = jnp.concatenate(
        [hi.astype(F32), mid.astype(F32), low.astype(F32), jnp.zeros((2, TOK), F32)], 0
    ).astype(BF16)
    sums = dot_nn(pieces, LT[...])
    cum = sums[0:2] + sums[2:4] + sums[4:6]
    total = cum[:, TOK - 1:]
    last_seg = seg[:, TOK - 1:]
    first_seg = seg[:, 0:1]
    tail = jnp.where(seg == last_seg, jnp.exp(total - cum), 0.0)
    enter = jnp.where(seg == first_seg, jnp.exp(cum), 0.0)
    colmat = jnp.concatenate([cum, seg, jnp.zeros((125, TOK), F32)], 0).T

    tb = jnp.concatenate([tapbc_ref[...], jnp.zeros((120, 128), F32)], 0).T

    def conv(before, now, seg_before, seg_now, taps):
        both = jnp.concatenate([before, now], 1)
        seg_both = jnp.broadcast_to(
            jnp.concatenate([seg_before, seg_now], 1), (8, both.shape[1])
        )
        total_sum = taps[:, 3:4] * now
        for off in (1, 2, 3):
            same = pltpu.roll(seg_both, off, 1)[0:1, 128:] == seg_now
            moved = pltpu.roll(both, off, 1)[:, 128:]
            total_sum = total_sum + taps[:, 3 - off:4 - off] * jnp.where(same, moved, 0.0)
        return silu(total_sum)

    def rounded(v):
        return v.astype(BF16).astype(F32)

    @pl.when(blk > 0)
    def _():
        arrive(HXR, RH.at[0])

    halo = HXR[...].astype(F32)
    seg_halo = halo[256:257, :]
    xin = conv(halo[0:128], rounded(ACC[128:256, :]), seg_halo, seg, smt)
    bcin = conv(halo[128:256], rounded(ACC[256:384, :]), seg_halo, seg, tb)
    bt = bcin[0:64].astype(BF16)
    ct = bcin[64:128].astype(BF16)

    def by_head(v):
        return jnp.concatenate(
            [jnp.broadcast_to(v[0:1], (64, TOK)), jnp.broadcast_to(v[1:2], (64, TOK))], 0
        )

    xdt = xin * by_head(step)
    state = dot_nt(bt, (xdt * by_head(tail)).astype(BF16))
    lane = lax.broadcasted_iota(jnp.int32, (1, 128), 1)
    tot_lane = jnp.where(lane < 64, total[0:1], total[1:2])
    hi, mid, low = three_parts(tot_lane)
    STS[0:64, :] = state.astype(BF16)
    STS[64:80, :] = jnp.concatenate(
        [hi.astype(F32), mid.astype(F32), low.astype(F32),
         jnp.broadcast_to(last_seg, (13, 128))], 0
    ).astype(BF16)
    st_sends = []
    for k in range(1, 8):
        st_sends.append(
            pltpu.make_async_remote_copy(
                src_ref=STS, dst_ref=STR.at[k - 1], send_sem=SS.at[kh + k],
                recv_sem=RS.at[k - 1], device_id=chain((blk + k) % 8), device_id_type=MESH,
            )
        )

        @pl.when(blk + k < 8)
        def _(k=k):
            st_sends[k - 1].start()

    xb = xdt.astype(BF16)
    yacc = [[None, None], [None, None]]
    for si, ti in ((0, 0), (0, 1), (1, 1)):
        ss, ts = slice(256 * si, 256 * si + 256), slice(256 * ti, 256 * ti + 256)
        scores = dot_tn(bt[:, ss], ct[:, ts])
        seen = colmat[ss, 2:3] == seg[:, ts]
        if si == ti:
            seen = seen & (
                lax.broadcasted_iota(jnp.int32, (256, 256), 0)
                <= lax.broadcasted_iota(jnp.int32, (256, 256), 1)
            )
        for h in (0, 1):
            gap = jnp.where(seen, cum[h:h + 1, ts] - colmat[ss, h:h + 1], -jnp.inf)
            mat = (jnp.exp(gap) * scores).astype(BF16)
            part = dot_nn(xb[64 * h:64 * h + 64, ss], mat)
            yacc[ti][h] = part if yacc[ti][h] is None else yacc[ti][h] + part
    inner = jnp.concatenate(
        [jnp.concatenate(yacc[0], 0), jnp.concatenate(yacc[1], 0)], 1
    )
    ACC[128:256, :] = inner + smt[:, 5:6] * xin

    ACC[256:320, 0:128] = jnp.zeros((64, 128), F32)
    ACC[320:328, 0:128] = jnp.zeros((8, 128), F32)
    for k in range(1, 8):
        @pl.when(blk >= k)
        def _(k=k):
            arrive(STR.at[k - 1], RS.at[k - 1])
            got = STR[k - 1].astype(F32)
            run = ACC[320:321, 0:128]
            weight = jnp.where(got[67:68] == first_seg, jnp.exp(run), 0.0)
            ACC[256:320, 0:128] += weight * got[0:64]
            ACC[320:321, 0:128] = run + (got[64:65] + got[65:66] + got[66:67])

    state_in = ACC[256:320, 0:128].astype(BF16)
    yout = ACC[128:256, :] + dot_tn(state_in, ct) * by_head(enter)
    gated = yout * silu(rounded(ACC[0:128, :]))
    scaled = gated * smt[:, 4:5]
    squares = gated * gated
    for j in range(4):
        js = slice(128 * j, 128 * j + 128)
        gj = scaled[:, js].T.astype(BF16)
        qj = squares[:, js].T.astype(BF16)
        for par in (0, 1):
            ps = slice(64 * par, 64 * par + 64)
            GN[c, j, par, :, 0:128] = gj[ps]
            GN[c, j, par, :, 128:256] = qj[ps]
    send(GN.at[c, :, 1 - c], GN.at[c, :, 1 - c], RN.at[0], core)

    @pl.when(foreign)
    def _():
        arrive(wo_at(2, 0, 64), RO.at[3])
        arrive(wo_at(2, 64, 64), RO.at[4])
        o_core.start()

    l_wo.wait()

    @pl.when(native)
    def _():
        arrive(WO.at[other, :], RO.at[5])

    arrive(GN.at[1 - c, :, c], RN.at[0])

    def product(wj):
        j = m4(wj)
        a = GN[0, j, c]
        b = GN[1, j, c]
        lhs = jnp.concatenate([a[:, 0:128], b[:, 0:128]], 1)
        for n in range(7):
            ns = slice(512 * n, 512 * n + 512)
            res = dot_nn(lhs, WO[:, ns]).astype(BF16)
            for r in range(4):
                PS[j, r, :, ns] = res[16 * r:16 * r + 16]
        sq = (a[:, 128:256].astype(F32) + b[:, 128:256].astype(F32)).astype(BF16)
        for r in range(4):
            PS[j, r, :, DEPTH:] = sq[16 * r:16 * r + 16]

    def chunk(wj, xj):
        return PS.at[m4(wj), m4(xj)]

    def outward(wj):
        j = m4(wj)
        product(wj)
        send(chunk(wj, x + 2), RXF.at[j], RX.at[0, j], dx(sgn))
        send(chunk(wj, x - sgn), RXS.at[j], RX.at[2, j], dx(-sgn))

    def combine(wj):
        j = m4(wj)
        arrive(RXF.at[j], RX.at[0, j])
        r = m4(x + sgn)
        PS[j, r] = (PS[j, r].astype(F32) + RXF[j].astype(F32)).astype(BF16)
        send(chunk(wj, x + sgn), RXC.at[j], RX.at[1, j], dx(sgn))

    def summed(wj):
        j = m4(wj)
        arrive(RXC.at[j], RX.at[1, j])
        arrive(RXS.at[j], RX.at[2, j])
        return PS[j, x].astype(F32) + RXC[j].astype(F32) + RXS[j].astype(F32)

    outward(w + 2)
    outward(w + sgn)
    combine(w + 2)
    outward(w - sgn)
    combine(w + sgn)
    outward(w)
    combine(w - sgn)
    PS[m4(w + 2), x] = summed(w + 2).astype(BF16)
    send(chunk(w + 2, x), RZF, RZ.at[0], dw(sgn))
    combine(w)
    part = summed(w + sgn)
    arrive(RZF, RZ.at[0])
    PS[m4(w + sgn), x] = (part + RZF[...].astype(F32)).astype(BF16)
    send(chunk(w + sgn, x), RZC, RZ.at[1], dw(sgn))
    PS[m4(w - sgn), x] = summed(w - sgn).astype(BF16)
    send(chunk(w - sgn, x), RZS, RZ.at[2], dw(-sgn))
    part = summed(w)
    arrive(RZC, RZ.at[1])
    arrive(RZS, RZ.at[2])
    full = part + RZC[...].astype(F32) + RZS[...].astype(F32)
    mean = jnp.sum(full[:, DEPTH:], axis=1, keepdims=True) / 4096.0
    result = (full[:, 0:DEPTH] * lax.rsqrt(mean + NORM_EPS)).astype(BF16)
    kf = count[0]
    count[0] += 1
    f_send = pltpu.make_async_remote_copy(
        src_ref=FS, dst_ref=FR, send_sem=SS.at[kf], recv_sem=RF.at[0],
        device_id=swap, device_id_type=MESH,
    )

    @pl.when(foreign)
    def _():
        FS[...] = result
        f_send.start()

    @pl.when(native)
    def _():
        out_ref[...] = result

    for cp in pending:
        cp.wait_send()

    @pl.when(native)
    def _():
        s_seg.wait_send()
        s_wz.wait_send()
        s_wd.wait_send()
        s_sm.wait_send()
        o_first.wait_send()

    @pl.when(foreign)
    def _():
        s_swap.wait_send()
        for cp in (w_up, w_down, w_fg, w_fi, o_up, o_down, o_fg, o_fi, o_core):
            cp.wait_send()
        arrive(FR, RF.at[0])
        out_ref[...] = FR[...]
        f_send.wait_send()

    @pl.when(blk < 7)
    def _():
        h_send.wait_send()

    for k in range(1, 8):
        @pl.when(blk + k < 8)
        def _(k=k):
            st_sends[k - 1].wait_send()


def local(
    tokens, w_zx, w_bc, w_dt, dt_bias, a_rate, d_skip, conv_x, conv_bc, norm_gain, w_out, segments
):
    def wide(v):
        return jnp.pad(v, (0, 126))[None]

    small = jnp.concatenate(
        [conv_x, norm_gain[None], jnp.repeat(d_skip, 64)[None], wide(dt_bias), wide(a_rate)], 0
    )
    tapbc = jnp.pad(conv_bc, ((0, 4), (0, 0)))
    anywhere = pl.BlockSpec(memory_space=pl.ANY)
    inside = pl.BlockSpec(memory_space=pltpu.VMEM)
    dma = pltpu.SemaphoreType.DMA
    return pl.pallas_call(
        kernel,
        out_shape=jax.ShapeDtypeStruct((16, DEPTH), BF16),
        in_specs=[anywhere] * 5 + [inside] + [anywhere] * 2,
        out_specs=inside,
        scratch_shapes=[
            pltpu.VMEM((DEPTH, TOK), BF16),
            pltpu.VMEM((2, DEPTH, 128), BF16),
            pltpu.VMEM((DEPTH, 128), BF16),
            pltpu.VMEM((2, DEPTH), BF16),
            pltpu.VMEM((8, 128), F32),
            pltpu.VMEM((1, TOK), jnp.int32),
            pltpu.VMEM((256, DEPTH), BF16),
            pltpu.VMEM((384, TOK), F32),
            pltpu.VMEM((TOK, TOK), BF16),
            pltpu.VMEM((272, 128), BF16),
            pltpu.VMEM((272, 128), BF16),
            pltpu.VMEM((80, 128), BF16),
            pltpu.VMEM((7, 80, 128), BF16),
            pltpu.VMEM((2, 4, 2, 64, 256), BF16),
            pltpu.VMEM((4, 4, 16, WIDE), BF16),
            pltpu.VMEM((4, 16, WIDE), BF16),
            pltpu.VMEM((4, 16, WIDE), BF16),
            pltpu.VMEM((4, 16, WIDE), BF16),
            pltpu.VMEM((16, WIDE), BF16),
            pltpu.VMEM((16, WIDE), BF16),
            pltpu.VMEM((16, WIDE), BF16),
            pltpu.VMEM((16, DEPTH), BF16),
            pltpu.VMEM((16, DEPTH), BF16),
            dma((96,)),
            dma((32,)),
            dma((5,)),
            dma((6,)),
            dma((3,)),
            dma((1,)),
            dma((7,)),
            dma((1,)),
            dma((1,)),
            dma((1,)),
            dma((3, 4)),
            dma((3,)),
            dma((7,)),
        ],
        compiler_params=pltpu.CompilerParams(
            collective_id=0, has_side_effects=True, vmem_limit_bytes=48 * 1024 * 1024
        ),
        cost_estimate=pl.CostEstimate(
            flops=2 * TOK * DEPTH * 512, bytes_accessed=10_000_000, transcendentals=500_000
        ),
    )(tokens.T, w_zx, w_bc, w_dt.T, small, tapbc, w_out, segments.reshape(1, TOK))


def solution(mesh):
    in_specs = (
        P("seq", "tensor"),
        P(None, None, "tensor"),
        P(),
        P(None, "tensor"),
        P("tensor"),
        P("tensor"),
        P("tensor"),
        P(None, "tensor"),
        P(),
        P("tensor"),
        P("tensor", None),
        P("seq"),
    )
    out_specs = P(("seq", "tensor"), None)
    return jax.shard_map(local, mesh=mesh, in_specs=in_specs, out_specs=out_specs, check_vma=False)
```

```python
import jax
import jax.numpy as jnp
from jax import lax
from jax.experimental import pallas as pl
from jax.experimental.pallas import tpu as pltpu
from jax.sharding import PartitionSpec as P

NORM_EPS = 1e-05
TOK = 512
FEAT = 112
DEPTH = 3584
QUART = DEPTH // 4
WIDE = DEPTH + 128
HALF = 256
MESH = pl.DeviceIdType.MESH
F32 = jnp.float32
BF16 = jnp.bfloat16


def silu(v):
    return v / (1.0 + jnp.exp(-v))


def softplus(v):
    return jnp.maximum(v, 0.0) + jnp.log1p(jnp.exp(-jnp.abs(v)))


def dot_tn(a, b):
    return lax.dot_general(a, b, (((0,), (0,)), ((), ())), preferred_element_type=F32)


def dot_nt(a, b):
    return lax.dot_general(a, b, (((1,), (1,)), ((), ())), preferred_element_type=F32)


def dot_nn(a, b):
    return jnp.dot(a, b, preferred_element_type=F32)


def three_parts(v):
    hi = v.astype(BF16)
    rest = v - hi.astype(F32)
    mid = rest.astype(BF16)
    low = (rest - mid.astype(F32)).astype(BF16)
    return hi, mid, low


def kernel(
    tok_hbm, wzx_hbm, wbc_hbm, wdt_hbm, tap_hbm, gain_hbm, bias_hbm, rate_hbm, skip_hbm, tapbc_hbm,
    wout_hbm, seg_hbm,
    out_ref,
    G, WZ, WB, WD, TAP, GAIN, BIAS, RATE, SKIP, TBC, SEG, WO, ACC, LT, HXS, HXR, STS, STR, GN, PS,
    RXF, RXC, RXS, RZF, RZC, RZS, FS, FR,
    SS, RG, RW, RO, RM, RH, RS, RN, RF, RC, RX, RZ, LC,
):
    seq, ten = lax.axis_index("seq"), lax.axis_index("tensor")
    y, c = seq // 2, seq % 2
    z, x = ten // 4, ten % 4
    w, kap = z // 2, z % 2
    blk = 2 * y + kap
    sgn = 1 - 2 * c
    native = c == kap
    foreign = c != kap

    def m4(v):
        return (v + 8) % 4

    def dev(yy, zz, xx, cc):
        return (2 * yy + cc, 4 * zz + xx)

    core = dev(y, z, x, 1 - c)

    def dx(k):
        return dev(y, z, m4(x + k), c)

    def dw(k):
        return dev(y, 2 * m4(w + k) + kap, x, c)

    def dy(k):
        return dev(m4(y + k), z, x, c)

    other_z = z + 1 - 2 * kap
    swap = dev(y, other_z, x, 1 - c)
    twin = dev(y, other_z, x, c)

    def chain(b):
        return dev(b // 2, 2 * w + b % 2, x, c)

    count = [0]
    pending = []

    def send(src, dst, rsem, device, track=True):
        k = count[0]
        count[0] += 1
        cp = pltpu.make_async_remote_copy(
            src_ref=src, dst_ref=dst, send_sem=SS.at[k], recv_sem=rsem,
            device_id=device, device_id_type=MESH,
        )
        cp.start()
        if track:
            pending.append(cp)
        return cp

    def arrive(dst, rsem):
        pltpu.make_async_remote_copy(
            src_ref=dst, dst_ref=dst, send_sem=SS.at[0], recv_sem=rsem,
            device_id=core, device_id_type=MESH,
        ).wait_recv()

    def gslot(f):
        return G.at[pl.ds(pl.multiple_of(f * FEAT, 16), FEAT), :]

    def fid(wj, xj, cc):
        return 8 * m4(wj) + 4 * cc + m4(xj)

    def gsend(wj, xj, device):
        f = fid(wj, xj, c)
        send(gslot(f), gslot(f), RG.at[f], device)

    def gwait(wj, xj, cc):
        f = fid(wj, xj, cc)
        arrive(gslot(f), RG.at[f])

    def orow(par):
        return pl.ds(pl.multiple_of(128 * par, 128), 128)

    own_f = fid(w, x, c)
    l_wb = pltpu.make_async_copy(wbc_hbm, WB, LC.at[0])
    l_wo = pltpu.make_async_copy(wout_hbm, WO.at[orow(kap), :], LC.at[1])
    l_tok = pltpu.make_async_copy(tok_hbm, gslot(own_f), LC.at[2])
    l_wz = pltpu.make_async_copy(wzx_hbm, WZ, LC.at[3])
    l_wd = pltpu.make_async_copy(wdt_hbm, WD, LC.at[4])
    l_tb = pltpu.make_async_copy(tapbc_hbm, TBC, LC.at[5])
    smalls = (
        (tap_hbm, TAP), (gain_hbm, GAIN), (bias_hbm, BIAS), (rate_hbm, RATE), (skip_hbm, SKIP)
    )
    l_sm = [pltpu.make_async_copy(a, v, LC.at[7 + i]) for i, (a, v) in enumerate(smalls)]
    l_sg = pltpu.make_async_copy(seg_hbm, SEG, LC.at[6])

    @pl.when(native)
    def _():
        l_tok.start()
        l_sg.start()
        l_wz.start()
        l_wd.start()
        for cp in l_sm:
            cp.start()

    l_tb.start()
    l_wb.start()
    l_wo.start()

    barrier = pltpu.get_barrier_semaphore()
    peers = [core, dx(1), dx(3), dw(1), dw(3), swap]
    peers += [chain((blk + k) % 8) for k in range(1, 8)]
    for p in peers:
        pl.semaphore_signal(barrier, inc=1, device_id=p, device_id_type=MESH)
    rows = lax.broadcasted_iota(jnp.int32, (TOK, TOK), 0)
    cols = lax.broadcasted_iota(jnp.int32, (TOK, TOK), 1)
    LT[...] = jnp.where(rows <= cols, 1.0, 0.0).astype(BF16)
    pl.semaphore_wait(barrier, len(peers))

    quart = pl.ds(pl.multiple_of(y * QUART, 128), QUART)

    def qrow(k):
        return pl.ds(pl.multiple_of(m4(y + k) * QUART, 128), QUART)

    k0 = count[0]
    count[0] += 8

    def sp_send(k, src, dst, rsem, device):
        return pltpu.make_async_remote_copy(
            src_ref=src, dst_ref=dst, send_sem=SS.at[k0 + k], recv_sem=rsem,
            device_id=device, device_id_type=MESH,
        )

    f_swap = fid(w, x, 1 - c)
    s_swap = sp_send(0, tok_hbm, gslot(f_swap), RG.at[f_swap], swap)
    s_seg = sp_send(0, seg_hbm, SEG, RM.at[2], core)
    s_wz = sp_send(1, wzx_hbm.at[:, quart, :], WZ.at[:, quart, :], RW.at[0], twin)
    s_wd = sp_send(2, wdt_hbm, WD, RM.at[0], twin)
    s_sm = [
        sp_send(3 + i, a, v, RM.at[3 + i], twin) for i, (a, v) in enumerate(smalls)
    ]

    @pl.when(foreign)
    def _():
        s_swap.start()
        gwait(w, x, c)

    @pl.when(native)
    def _():
        s_seg.start()
        l_tok.wait()

    gsend(w, x, dw(1))
    gsend(w, x, dw(3))
    gsend(w, x, dx(1))
    gsend(w, x, dx(3))
    gsend(w, x, core)

    @pl.when(native)
    def _():
        s_wd.start()
        for cp in s_sm:
            cp.start()
        s_wz.start()

    def pass_x(wj):
        gwait(wj, x - sgn, c)
        gsend(wj, x - sgn, dx(sgn))
        gsend(wj, x - sgn, core)

    def spread_x(wj):
        gsend(wj, x, dx(1))
        gsend(wj, x, dx(3))
        gsend(wj, x, core)

    def to_core(wj, xj):
        gwait(wj, xj, c)
        gsend(wj, xj, core)

    pass_x(w)
    gwait(w - sgn, x, c)
    gsend(w - sgn, x, dw(sgn))
    spread_x(w - sgn)
    gwait(w + sgn, x, c)
    spread_x(w + sgn)
    to_core(w, x + sgn)

    kw = count[0]
    count[0] += 10

    def wsend(k, src, dst, rsem, device):
        return pltpu.make_async_remote_copy(
            src_ref=src, dst_ref=dst, send_sem=SS.at[kw + k], recv_sem=rsem,
            device_id=device, device_id_type=MESH,
        )

    def wz_at(k):
        return WZ.at[:, qrow(k), :]

    w_up = wsend(0, wz_at(0), wz_at(0), RW.at[1], dy(1))
    w_down = wsend(1, wz_at(0), wz_at(0), RW.at[2], dy(3))
    w_fg = wsend(2, WZ.at[0, qrow(-1), :], WZ.at[0, qrow(-1), :], RW.at[3], dy(1))
    w_fi = wsend(3, WZ.at[1, qrow(1), :], WZ.at[1, qrow(1), :], RW.at[4], dy(3))
    other = orow(1 - kap)

    def wo_at(k, lo=0, n=128):
        return WO.at[pl.ds(pl.multiple_of(128 * (1 - kap) + lo, 64), n), qrow(k)]

    o_first = wsend(
        4, wout_hbm.at[:, quart], WO.at[orow(kap), quart], RO.at[0], twin
    )
    o_up = wsend(4, wo_at(0), wo_at(0), RO.at[1], dy(1))
    o_down = wsend(5, wo_at(0), wo_at(0), RO.at[2], dy(3))
    o_fg = wsend(6, wo_at(-1, 0, 64), wo_at(-1, 0, 64), RO.at[3], dy(1))
    o_fi = wsend(7, wo_at(1, 64, 64), wo_at(1, 64, 64), RO.at[4], dy(3))
    o_core = wsend(8, WO.at[other, :], WO.at[other, :], RO.at[5], core)

    @pl.when(foreign)
    def _():
        arrive(wz_at(0), RW.at[0])
        w_up.start()
        w_down.start()

    pass_x(w - sgn)
    pass_x(w + sgn)
    gwait(w + 2, x, c)
    spread_x(w + 2)

    @pl.when(native)
    def _():
        o_first.start()

    to_core(w, x + 2)
    to_core(w - sgn, x + sgn)
    to_core(w + sgn, x + sgn)
    pass_x(w + 2)

    @pl.when(foreign)
    def _():
        arrive(wz_at(-1), RW.at[1])
        w_fg.start()
        arrive(wz_at(1), RW.at[2])
        w_fi.start()
        arrive(wo_at(0), RO.at[0])
        o_up.start()
        o_down.start()

    to_core(w - sgn, x + 2)
    to_core(w + sgn, x + 2)
    to_core(w + 2, x + sgn)
    to_core(w + 2, x + 2)

    @pl.when(foreign)
    def _():
        arrive(WZ.at[0, qrow(2), :], RW.at[3])
        arrive(WZ.at[1, qrow(2), :], RW.at[4])
        arrive(WD, RM.at[0])
        for i, (_, v) in enumerate(smalls):
            arrive(v, RM.at[3 + i])
        arrive(SEG, RM.at[2])

    @pl.when(native)
    def _():
        l_wz.wait()
        l_wd.wait()
        for cp in l_sm:
            cp.wait()
        l_sg.wait()

    l_wb.wait()
    l_tb.wait()

    for i, wj in enumerate((w, w - sgn, w + sgn, w + 2)):
        for xj in range(4):
            gwait(wj, xj, 1 - c)
        krow = pl.ds(pl.multiple_of(m4(wj) * QUART, 128), QUART)
        gk = G[krow, :]
        parts = (
            dot_tn(WZ[0, krow, :], gk),
            dot_tn(WZ[1, krow, :], gk),
            dot_tn(WB[krow, :], gk),
        )
        for j, part in enumerate(parts):
            at = slice(128 * j, 128 * j + 128)
            ACC[at, :] = part if i == 0 else ACC[at, :] + part

    dt_raw = dot_nn(WD[...], G[...])

    @pl.when(foreign)
    def _():
        arrive(wo_at(-1), RO.at[1])
        o_fg.start()
        arrive(wo_at(1), RO.at[2])
        o_fi.start()

    seg = SEG[...].astype(F32)
    HXS[0:256, :] = ACC[128:384, TOK - 128:].astype(BF16)
    HXS[256:272, :] = jnp.broadcast_to(seg[:, TOK - 128:], (16, 128)).astype(BF16)
    kh = count[0]
    count[0] += 8
    h_send = pltpu.make_async_remote_copy(
        src_ref=HXS, dst_ref=HXR, send_sem=SS.at[kh], recv_sem=RH.at[0],
        device_id=chain((blk + 1) % 8), device_id_type=MESH,
    )

    @pl.when(blk < 7)
    def _():
        h_send.start()

    @pl.when(blk == 0)
    def _():
        HXR[0:256, :] = jnp.zeros((256, 128), BF16)
        HXR[256:272, :] = jnp.full((16, 128), -1.0, BF16)

    lane = lax.broadcasted_iota(jnp.int32, (1, 128), 1)

    def two_rows(ref):
        v = ref[...]
        return jnp.concatenate([v[:, 0:1], v[:, 1:2]], 0)

    skip = SKIP[...]
    skip_lane = jnp.where(lane < 64, skip[:, 0:1], skip[:, 1:2])
    smt = jnp.concatenate([TAP[...], GAIN[...], skip_lane, jnp.zeros((122, 128), F32)], 0).T
    step = softplus(dt_raw + two_rows(BIAS))
    logdec = -two_rows(RATE) * step
    hi, mid, low = three_parts(logdec)
    pieces = jnp.concatenate(
        [hi.astype(F32), mid.astype(F32), low.astype(F32), jnp.zeros((2, TOK), F32)], 0
    ).astype(BF16)
    sums = dot_nn(pieces, LT[...])
    cum = sums[0:2] + sums[2:4] + sums[4:6]
    total = cum[:, TOK - 1:]
    last_seg = seg[:, TOK - 1:]
    first_seg = seg[:, 0:1]
    tail = jnp.where(seg == last_seg, jnp.exp(total - cum), 0.0)
    enter = jnp.where(seg == first_seg, jnp.exp(cum), 0.0)
    colmat = jnp.concatenate([cum, seg, jnp.zeros((125, TOK), F32)], 0).T

    tb = jnp.concatenate([TBC[...], jnp.zeros((124, 128), F32)], 0).T

    def conv(before, now, seg_before, seg_now, taps):
        both = jnp.concatenate([before, now], 1)
        seg_both = jnp.broadcast_to(
            jnp.concatenate([seg_before, seg_now], 1), (8, both.shape[1])
        )
        total_sum = taps[:, 3:4] * now
        for off in (1, 2, 3):
            same = pltpu.roll(seg_both, off, 1)[0:1, 128:] == seg_now
            moved = pltpu.roll(both, off, 1)[:, 128:]
            total_sum = total_sum + taps[:, 3 - off:4 - off] * jnp.where(same, moved, 0.0)
        return silu(total_sum)

    def rounded(v):
        return v.astype(BF16).astype(F32)

    @pl.when(blk > 0)
    def _():
        arrive(HXR, RH.at[0])

    halo = HXR[...].astype(F32)
    seg_halo = halo[256:257, :]
    xin = conv(halo[0:128], rounded(ACC[128:256, :]), seg_halo, seg, smt)
    bcin = conv(halo[128:256], rounded(ACC[256:384, :]), seg_halo, seg, tb)
    bt = bcin[0:64].astype(BF16)
    ct = bcin[64:128].astype(BF16)

    def by_head(v):
        return jnp.concatenate(
            [jnp.broadcast_to(v[0:1], (64, TOK)), jnp.broadcast_to(v[1:2], (64, TOK))], 0
        )

    xdt = xin * by_head(step)
    state = dot_nt(bt, (xdt * by_head(tail)).astype(BF16))
    tot_lane = jnp.where(lane < 64, total[0:1], total[1:2])
    hi, mid, low = three_parts(tot_lane)
    STS[0:64, :] = state.astype(BF16)
    STS[64:80, :] = jnp.concatenate(
        [hi.astype(F32), mid.astype(F32), low.astype(F32),
         jnp.broadcast_to(last_seg, (13, 128))], 0
    ).astype(BF16)
    st_sends = []
    for k in range(1, 8):
        st_sends.append(
            pltpu.make_async_remote_copy(
                src_ref=STS, dst_ref=STR.at[k - 1], send_sem=SS.at[kh + k],
                recv_sem=RS.at[k - 1], device_id=chain((blk + k) % 8), device_id_type=MESH,
            )
        )

        @pl.when(blk + k < 8)
        def _(k=k):
            st_sends[k - 1].start()

    xb = xdt.astype(BF16)
    yacc = [[None, None], [None, None]]
    for si, ti in ((0, 0), (0, 1), (1, 1)):
        ss, ts = slice(256 * si, 256 * si + 256), slice(256 * ti, 256 * ti + 256)
        scores = dot_tn(bt[:, ss], ct[:, ts])
        seen = colmat[ss, 2:3] == seg[:, ts]
        if si == ti:
            seen = seen & (
                lax.broadcasted_iota(jnp.int32, (256, 256), 0)
                <= lax.broadcasted_iota(jnp.int32, (256, 256), 1)
            )
        for h in (0, 1):
            gap = jnp.where(seen, cum[h:h + 1, ts] - colmat[ss, h:h + 1], -jnp.inf)
            mat = (jnp.exp(gap) * scores).astype(BF16)
            part = dot_nn(xb[64 * h:64 * h + 64, ss], mat)
            yacc[ti][h] = part if yacc[ti][h] is None else yacc[ti][h] + part
    inner = jnp.concatenate(
        [jnp.concatenate(yacc[0], 0), jnp.concatenate(yacc[1], 0)], 1
    )
    ACC[128:256, :] = inner + smt[:, 5:6] * xin

    ACC[256:320, 0:128] = jnp.zeros((64, 128), F32)
    ACC[320:328, 0:128] = jnp.zeros((8, 128), F32)
    for k in range(1, 8):
        @pl.when(blk >= k)
        def _(k=k):
            arrive(STR.at[k - 1], RS.at[k - 1])
            got = STR[k - 1].astype(F32)
            run = ACC[320:321, 0:128]
            weight = jnp.where(got[67:68] == first_seg, jnp.exp(run), 0.0)
            ACC[256:320, 0:128] += weight * got[0:64]
            ACC[320:321, 0:128] = run + (got[64:65] + got[65:66] + got[66:67])

    state_in = ACC[256:320, 0:128].astype(BF16)
    yout = ACC[128:256, :] + dot_tn(state_in, ct) * by_head(enter)
    gated = yout * silu(rounded(ACC[0:128, :]))
    scaled = gated * smt[:, 4:5]
    squares = gated * gated
    for j in range(4):
        js = slice(128 * j, 128 * j + 128)
        gj = scaled[:, js].T.astype(BF16)
        qj = squares[:, js].T.astype(BF16)
        for par in (0, 1):
            ps = slice(64 * par, 64 * par + 64)
            GN[c, j, par, :, 0:128] = gj[ps]
            GN[c, j, par, :, 128:256] = qj[ps]
    send(GN.at[c, :, 1 - c], GN.at[c, :, 1 - c], RN.at[0], core)

    @pl.when(foreign)
    def _():
        arrive(wo_at(2, 0, 64), RO.at[3])
        arrive(wo_at(2, 64, 64), RO.at[4])
        o_core.start()

    l_wo.wait()

    @pl.when(native)
    def _():
        arrive(WO.at[other, :], RO.at[5])

    arrive(GN.at[1 - c, :, c], RN.at[0])

    def product(wj):
        j = m4(wj)
        a = GN[0, j, c]
        b = GN[1, j, c]
        lhs = jnp.concatenate([a[:, 0:128], b[:, 0:128]], 1)
        for n in range(7):
            ns = slice(512 * n, 512 * n + 512)
            res = dot_nn(lhs, WO[:, ns]).astype(BF16)
            for r in range(4):
                PS[j, r, :, ns] = res[16 * r:16 * r + 16]
        sq = (a[:, 128:256].astype(F32) + b[:, 128:256].astype(F32)).astype(BF16)
        for r in range(4):
            PS[j, r, :, DEPTH:] = sq[16 * r:16 * r + 16]

    def chunk(wj, xj):
        return PS.at[m4(wj), m4(xj)]

    def outward(wj):
        j = m4(wj)
        product(wj)
        send(chunk(wj, x + 2), RXF.at[j], RX.at[0, j], dx(sgn))
        send(chunk(wj, x - sgn), RXS.at[j], RX.at[2, j], dx(-sgn))

    def combine(wj):
        j = m4(wj)
        arrive(RXF.at[j], RX.at[0, j])
        r = m4(x + sgn)
        PS[j, r] = (PS[j, r].astype(F32) + RXF[j].astype(F32)).astype(BF16)
        send(chunk(wj, x + sgn), RXC.at[j], RX.at[1, j], dx(sgn))

    def summed(wj):
        j = m4(wj)
        arrive(RXC.at[j], RX.at[1, j])
        arrive(RXS.at[j], RX.at[2, j])
        return PS[j, x].astype(F32) + RXC[j].astype(F32) + RXS[j].astype(F32)

    outward(w + 2)
    outward(w + sgn)
    combine(w + 2)
    outward(w - sgn)
    combine(w + sgn)
    outward(w)
    combine(w - sgn)
    PS[m4(w + 2), x] = summed(w + 2).astype(BF16)
    send(chunk(w + 2, x), RZF, RZ.at[0], dw(sgn))
    combine(w)
    part = summed(w + sgn)
    arrive(RZF, RZ.at[0])
    PS[m4(w + sgn), x] = (part + RZF[...].astype(F32)).astype(BF16)
    send(chunk(w + sgn, x), RZC, RZ.at[1], dw(sgn))
    PS[m4(w - sgn), x] = summed(w - sgn).astype(BF16)
    send(chunk(w - sgn, x), RZS, RZ.at[2], dw(-sgn))
    part = summed(w)
    arrive(RZC, RZ.at[1])
    arrive(RZS, RZ.at[2])
    full = part + RZC[...].astype(F32) + RZS[...].astype(F32)
    mean = jnp.sum(full[:, DEPTH:], axis=1, keepdims=True) / 4096.0
    result = (full[:, 0:DEPTH] * lax.rsqrt(mean + NORM_EPS)).astype(BF16)
    kf = count[0]
    count[0] += 1
    f_send = pltpu.make_async_remote_copy(
        src_ref=FS, dst_ref=FR, send_sem=SS.at[kf], recv_sem=RF.at[0],
        device_id=swap, device_id_type=MESH,
    )

    @pl.when(foreign)
    def _():
        FS[...] = result
        f_send.start()

    @pl.when(native)
    def _():
        out_ref[...] = result

    for cp in pending:
        cp.wait_send()

    @pl.when(native)
    def _():
        s_seg.wait_send()
        s_wz.wait_send()
        s_wd.wait_send()
        for cp in s_sm:
            cp.wait_send()
        o_first.wait_send()

    @pl.when(foreign)
    def _():
        s_swap.wait_send()
        for cp in (w_up, w_down, w_fg, w_fi, o_up, o_down, o_fg, o_fi, o_core):
            cp.wait_send()
        arrive(FR, RF.at[0])
        out_ref[...] = FR[...]
        f_send.wait_send()

    @pl.when(blk < 7)
    def _():
        h_send.wait_send()

    for k in range(1, 8):
        @pl.when(blk + k < 8)
        def _(k=k):
            st_sends[k - 1].wait_send()


def local(
    tokens, w_zx, w_bc, w_dt, dt_bias, a_rate, d_skip, conv_x, conv_bc, norm_gain, w_out, segments
):
    outside = pl.BlockSpec(memory_space=pltpu.HBM)
    inside = pl.BlockSpec(memory_space=pltpu.VMEM)
    dma = pltpu.SemaphoreType.DMA
    return pl.pallas_call(
        kernel,
        out_shape=jax.ShapeDtypeStruct((16, DEPTH), BF16),
        in_specs=[outside] * 12,
        out_specs=inside,
        scratch_shapes=[
            pltpu.VMEM((DEPTH, TOK), BF16),
            pltpu.VMEM((2, DEPTH, 128), BF16),
            pltpu.VMEM((DEPTH, 128), BF16),
            pltpu.VMEM((2, DEPTH), BF16),
            pltpu.VMEM((4, 128), F32),
            pltpu.VMEM((1, 128), F32),
            pltpu.VMEM((1, 2), F32),
            pltpu.VMEM((1, 2), F32),
            pltpu.VMEM((1, 2), F32),
            pltpu.VMEM((4, 128), F32),
            pltpu.VMEM((1, TOK), jnp.int32),
            pltpu.VMEM((256, DEPTH), BF16),
            pltpu.VMEM((384, TOK), F32),
            pltpu.VMEM((TOK, TOK), BF16),
            pltpu.VMEM((272, 128), BF16),
            pltpu.VMEM((272, 128), BF16),
            pltpu.VMEM((80, 128), BF16),
            pltpu.VMEM((7, 80, 128), BF16),
            pltpu.VMEM((2, 4, 2, 64, 256), BF16),
            pltpu.VMEM((4, 4, 16, WIDE), BF16),
            pltpu.VMEM((4, 16, WIDE), BF16),
            pltpu.VMEM((4, 16, WIDE), BF16),
            pltpu.VMEM((4, 16, WIDE), BF16),
            pltpu.VMEM((16, WIDE), BF16),
            pltpu.VMEM((16, WIDE), BF16),
            pltpu.VMEM((16, WIDE), BF16),
            pltpu.VMEM((16, DEPTH), BF16),
            pltpu.VMEM((16, DEPTH), BF16),
            dma((96,)),
            dma((32,)),
            dma((5,)),
            dma((6,)),
            dma((8,)),
            dma((1,)),
            dma((7,)),
            dma((1,)),
            dma((1,)),
            dma((1,)),
            dma((3, 4)),
            dma((3,)),
            dma((12,)),
        ],
        compiler_params=pltpu.CompilerParams(
            collective_id=0, has_side_effects=True, vmem_limit_bytes=60 * 1024 * 1024
        ),
        cost_estimate=pl.CostEstimate(
            flops=2 * TOK * DEPTH * 512, bytes_accessed=10_000_000, transcendentals=500_000
        ),
    )(
        tokens.T, w_zx, w_bc, w_dt.T, conv_x, norm_gain.reshape(1, 128), dt_bias.reshape(1, 2),
        a_rate.reshape(1, 2), d_skip.reshape(1, 2), conv_bc, w_out, segments.reshape(1, TOK),
    )


def solution(mesh):
    in_specs = (
        P("seq", "tensor"),
        P(None, None, "tensor"),
        P(),
        P(None, "tensor"),
        P("tensor"),
        P("tensor"),
        P("tensor"),
        P(None, "tensor"),
        P(),
        P("tensor"),
        P("tensor", None),
        P("seq"),
    )
    out_specs = P(("seq", "tensor"), None)
    return jax.shard_map(local, mesh=mesh, in_specs=in_specs, out_specs=out_specs, check_vma=False)
```
